32 devices in a mesh: dom: 32 (over z, y, x, core).
Axes of the slice: x: 2, y: 2, z: 4, core: 2. Of those that a mesh axis runs over, the one named last changes fastest.
Arguments:
- z_state: bfloat16 [96, 262144], P(None, 'dom'), may hold values from 0 to 20, as said below
- inputs: bfloat16 [128, 262144], P(None, 'dom'), may hold values from -6 to 6
- adjoint: bfloat16 [96, 262144], P(None, 'dom'), may hold values from -6 to 6
- cotangent: bfloat16 [96, 262144], P(None, 'dom'), may hold values from -0.59765625 to 0.59765625
- mix_weight: bfloat16 [96, 96], replicated, may hold values from -0.625 to 0.625
- input_weight: bfloat16 [96, 128], replicated, may hold values from -0.5 to 0.5
- tile_values: bfloat16 [8192, 128, 128], P('dom'), may hold values from 0 to 0.019897461
- tile_src: int32 [32, 256], P('dom'), may hold values from 0 to 191, as said below
- tile_dst: int32 [32, 256], P('dom'), may hold values from 0 to 63
- send_list: int32 [32, 8, 16], P('dom'), may hold values from 0 to 63
Outputs:
- fixed_next: bfloat16 [96, 262144], P(None, 'dom')
- adjoint_next: bfloat16 [96, 262144], P(None, 'dom')
- weight_grad: float32 [96, 96], replicated
- input_grad: float32 [96, 128], replicated
The draws below stay inside these ranges and needn't reach their ends.
Inputs may be any that keep to these rules, and one draw needn't show every extreme that they name: `tile_src`: codes below 64 name a local tile; code 64 + o * 16 + c names slot c of neighbour o's list for this partition. Every code from 64 upward appears on every partition. `z_state`: zero or positive; a state after a rectifier.
All inputs are finite; a program needn't handle non-finite values.
Results may differ from the reference program's by a relative error of at most 0.0058.
Values may be sent and summed in bfloat16 or wider, within the bound.
A program may use at most 128 MiB of HBM per device.

```python
import math
import jax
import jax.numpy as jnp
from jax import lax

H = 96
F = 128
NODE_DEV = 8192
TILE = 128
REACH = 4
TILES_LOC = 64
CAP = 16
TILES_DEV = 256
NODES = 262144
TILES = 8192
N_DOM = 32


def draw_z_state(key, part):
    noise_key = jax.random.fold_in(jax.random.fold_in(key, 5), 0)
    values = jax.random.normal(noise_key, (H, NODES), jnp.float32)
    return jnp.maximum(values, 0.0).astype(jnp.bfloat16)


def draw_tile_src(key, part):
    local_tiles = NODE_DEV // TILE
    remote = 2 * REACH * CAP

    def one_device(device_key):
        fill_key, order_key = jax.random.split(device_key)
        fixed_codes = local_tiles + jnp.arange(remote, dtype=jnp.int32)
        further = jax.random.randint(fill_key, (TILES_DEV - remote,), 0, local_tiles + remote, dtype=jnp.int32)
        return jax.random.permutation(order_key, jnp.concatenate([fixed_codes, further]))
    device_keys = jax.random.split(jax.random.fold_in(key, 11), N_DOM)
    return jax.vmap(one_device)(device_keys)


def with_ends(drawn, own_key, low, largest):
    extent = drawn.shape
    index_at = [jax.random.randint(jax.random.fold_in(own_key, axis), (), 0, extent[axis]) for axis in range(len(extent))]
    drawn = drawn.at[tuple(index_at)].set(low)
    longest = extent.index(max(extent))
    index_at[longest] = (index_at[longest] + 1) % extent[longest]
    return drawn.at[tuple(index_at)].set(largest)


def block_scale(stream_key, shape, cuts, least, top_value):
    loudness, own = 1.0, jax.random.fold_in(stream_key, 6)
    for axis_at, parts in cuts:
        steps = jnp.exp(jax.random.uniform(jax.random.fold_in(own, axis_at), (parts,), jnp.float32, least / len(cuts), top_value / len(cuts)))
        loudness = loudness * jnp.repeat(steps, shape[axis_at] // parts).reshape([-1 if axis == axis_at else 1 for axis in range(len(shape))])
    return loudness


def scatter_about(own_key, shape, scale, reach, cuts=(), kind=jnp.bfloat16):
    level = block_scale(own_key, shape, cuts, -0.22, 0.18) if cuts else 1.0
    array = jax.random.normal(own_key, shape, jnp.float32) * scale * level
    return jnp.minimum(jnp.maximum(array, -reach), reach).astype(kind)


def setup_inputs(seed: int = 0) -> dict:
    key_list = jax.random.split(jax.random.key(seed), 11)
    return {
        "z_state": draw_z_state(jax.random.fold_in(key_list[10], 71), 0),
        "inputs": scatter_about(key_list[1], (F, NODES), 1.0, 6.0, ((1, 32),)),
        "adjoint": scatter_about(key_list[2], (H, NODES), 1.0, 6.0, ((1, 32),)),
        "cotangent": scatter_about(key_list[3], (H, NODES), 0.1, 0.59765625, ((1, 32),)),
        "mix_weight": scatter_about(key_list[4], (H, H), H ** -0.5, 0.625),
        "input_weight": scatter_about(key_list[5], (H, F), F ** -0.5, 0.5),
        "tile_values": jnp.clip(0.019897461 * jax.random.uniform(key_list[6], (TILES, TILE, TILE), jnp.float32) ** block_scale(key_list[6], (TILES, TILE, TILE), ((0, 32),), -0.2, 0.2), 0.0, 0.019897461).astype(jnp.bfloat16),
        "tile_src": draw_tile_src(jax.random.fold_in(key_list[10], 71), 0),
        "tile_dst": with_ends(jax.random.randint(key_list[8], (N_DOM, TILES_DEV), 0, TILES_LOC), jax.random.fold_in(key_list[8], 1), 0, TILES_LOC - 1).astype(jnp.int32),
        "send_list": with_ends(jax.random.randint(key_list[9], (N_DOM, 2 * REACH, CAP), 0, TILES_LOC), jax.random.fold_in(key_list[9], 1), 0, TILES_LOC - 1).astype(jnp.int32),
    }


highest = lax.Precision.HIGHEST

def peer_offsets():
    index = jnp.arange(2 * REACH, dtype=jnp.int32)
    return jnp.where(index < REACH, index + 1, REACH - 1 - index).astype(jnp.int32)

def global_sources(send_list, tile_src):
    devices = jnp.arange(N_DOM, dtype=jnp.int32)[:, None]
    remote = jnp.maximum(tile_src - TILES_LOC, 0).astype(jnp.int32)
    offset_index = (remote // CAP).astype(jnp.int32)
    slot_column = (remote % CAP).astype(jnp.int32)
    peer_device = ((devices - peer_offsets()[offset_index]) % N_DOM).astype(jnp.int32)
    far_tiles = peer_device * TILES_LOC + send_list[peer_device, offset_index, slot_column]
    near_tiles = devices * TILES_LOC + tile_src
    return jnp.where(tile_src < TILES_LOC, near_tiles, far_tiles).astype(jnp.int32)

def reference(z_state, inputs, adjoint, cotangent, mix_weight, input_weight, tile_values, tile_src, tile_dst, send_list):
    sources = global_sources(send_list, tile_src)
    blocks = tile_values.reshape(N_DOM, TILES_DEV, TILE, TILE)
    state_tiles = z_state.reshape(H, N_DOM * TILES_LOC, TILE)

    def forward_device(operands):
        source_ids, dest_ids, device_blocks = operands
        pieces = state_tiles[:, source_ids].astype(jnp.float32)
        contributions = jnp.einsum('hks,ksd->khd', pieces, device_blocks.astype(jnp.float32), precision=highest)
        return jax.ops.segment_sum(contributions, dest_ids, TILES_LOC)
    gathered = lax.map(forward_device, (sources, tile_dst, blocks))
    aggregated = jnp.moveaxis(gathered, 2, 0).reshape(H, NODES).astype(jnp.bfloat16)
    preactivation = jnp.dot(mix_weight, aggregated, preferred_element_type=jnp.float32) + jnp.dot(input_weight, inputs, preferred_element_type=jnp.float32)
    fixed_next = jnp.maximum(preactivation, 0.0).astype(jnp.bfloat16)
    masked = jnp.where(z_state > 0, adjoint, jnp.zeros_like(adjoint))
    backward = jnp.dot(mix_weight.T, masked, preferred_element_type=jnp.float32).astype(jnp.bfloat16)
    back_tiles = backward.reshape(H, N_DOM * TILES_LOC, TILE)

    def backward_device(running, operands):
        device, source_ids, dest_ids, device_blocks = operands
        pieces = back_tiles[:, device * TILES_LOC + dest_ids].astype(jnp.float32)
        partials = jnp.einsum('hkd,ksd->khs', pieces, device_blocks.astype(jnp.float32), precision=highest)
        return (running.at[source_ids].add(partials), None)
    start = jnp.zeros((N_DOM * TILES_LOC, H, TILE), jnp.float32)
    device_ids = jnp.arange(N_DOM, dtype=jnp.int32)
    summed, unused = lax.scan(backward_device, start, (device_ids, sources, tile_dst, blocks))
    adjoint_sum = jnp.moveaxis(summed, 1, 0).reshape(H, NODES)
    adjoint_next = (cotangent.astype(jnp.float32) + adjoint_sum).astype(jnp.bfloat16)
    normalizer = 1.0 / math.sqrt(NODES)
    weight_grad = jnp.dot(masked, aggregated.T, preferred_element_type=jnp.float32) * normalizer
    input_grad = jnp.dot(masked, inputs.T, preferred_element_type=jnp.float32) * normalizer
    return (fixed_next, adjoint_next, weight_grad, input_grad)
```

```python
import functools
import math

import jax
import jax.numpy as jnp
from jax import lax
from jax.experimental import pallas as pl
from jax.experimental.pallas import tpu as pltpu
from jax.sharding import PartitionSpec as P

MESH = pl.DeviceIdType.MESH
BLOCK = 16
LANES = 1024


def lane_slice(start, size):
    return pl.ds(pl.multiple_of(start, size), size)


def dot(a, b, contract):
    return lax.dot_general(a, b, (contract, ((), ())), preferred_element_type=jnp.float32)


def backward_kernel(
    src, dst, send, z_ref, adj_ref, x_ref, w_ref, a_ref,
    zout_ref, leave_ref, local_ref, ig_ref, back, acc,
):
    step = pl.program_id(0)
    tile = a_ref.shape[1]
    nodes = z_ref.shape[1]
    slots = zout_ref.shape[0]
    local_tiles = local_ref.shape[0]

    @pl.when(step == 0)
    def _():
        def gather(s, c):
            zout_ref[s] = z_ref[:, lane_slice(send[s] * tile, tile)]
            return c

        lax.fori_loop(0, slots, gather, 0)

        def clear(s, c):
            acc[s] = jnp.zeros(acc.shape[1:], acc.dtype)
            return c

        lax.fori_loop(0, acc.shape[0], clear, 0)
        ig_ref[...] = jnp.zeros_like(ig_ref)

        def chunk(i, c):
            at = lane_slice(i * LANES, LANES)
            adj = adj_ref[:, at]
            masked = jnp.where(z_ref[:, at] > 0, adj, jnp.zeros_like(adj))
            back[:, at] = dot(w_ref[...], masked, ((0,), (0,))).astype(back.dtype)
            ig_ref[...] += dot(masked, x_ref[:, at], ((1,), (1,)))
            return c

        lax.fori_loop(0, nodes // LANES, chunk, 0)

    for j in range(a_ref.shape[0]):
        k = step * a_ref.shape[0] + j
        piece = back[:, lane_slice(dst[k] * tile, tile)]
        acc[src[k]] += dot(piece, a_ref[j], ((1,), (1,)))

    @pl.when(step == pl.num_programs(0) - 1)
    def _():
        def keep(t, c):
            local_ref[t] = acc[t]
            return c

        lax.fori_loop(0, local_tiles, keep, 0)

        def leave(s, c):
            leave_ref[s] = acc[local_tiles + s].astype(leave_ref.dtype)
            return c

        lax.fori_loop(0, slots, leave, 0)


def exchange_kernel(n, offsets, zout, leave, zin, ret, send_sem, recv_sem):
    me = lax.axis_index("dom")
    barrier = pltpu.get_barrier_semaphore()
    for off in offsets:
        pl.semaphore_signal(
            barrier, inc=1, device_id=(lax.rem(me + off + n, n),), device_id_type=MESH
        )
    pl.semaphore_wait(barrier, len(offsets))
    cap = zout.shape[0] // len(offsets)
    copies = []
    for kind, (src, dst, sign) in enumerate(((zout, zin, 1), (leave, ret, -1))):
        for o, off in enumerate(offsets):
            at = pl.ds(o * cap, cap)
            copies.append(
                pltpu.make_async_remote_copy(
                    src_ref=src.at[at],
                    dst_ref=dst.at[at],
                    send_sem=send_sem.at[kind, o],
                    recv_sem=recv_sem.at[kind, o],
                    device_id=(lax.rem(me + sign * off + n, n),),
                    device_id_type=MESH,
                )
            )
    for copy in copies:
        copy.start()
    for copy in copies:
        copy.wait()


def forward_kernel(
    src, dst, send, z_ref, adj_ref, cot_ref, x_ref, w_ref, b_ref, zin_ref, ret_ref, local_ref,
    a_ref, fixed_ref, next_ref, wg_ref, table, acc, own,
):
    step = pl.program_id(0)
    tile = a_ref.shape[1]
    nodes = z_ref.shape[1]
    slots = zin_ref.shape[0]
    local_tiles = acc.shape[0]

    @pl.when(step == 0)
    def _():
        def fill(t, c):
            at = lane_slice(t * tile, tile)
            table[t] = z_ref[:, at]
            acc[t] = jnp.zeros(acc.shape[1:], acc.dtype)
            own[t] = local_ref[t] + cot_ref[:, at].astype(jnp.float32)
            return c

        lax.fori_loop(0, local_tiles, fill, 0)

        def fill_in(s, c):
            table[local_tiles + s] = zin_ref[s]
            own[send[s]] += ret_ref[s].astype(jnp.float32)
            return c

        lax.fori_loop(0, slots, fill_in, 0)

    for j in range(a_ref.shape[0]):
        k = step * a_ref.shape[0] + j
        acc[dst[k]] += dot(table[src[k]], a_ref[j], ((1,), (0,)))

    @pl.when(step == pl.num_programs(0) - 1)
    def _():
        per = LANES // tile
        wg_ref[...] = jnp.zeros_like(wg_ref)

        def chunk(i, c):
            at = lane_slice(i * LANES, LANES)
            agg = jnp.concatenate(
                [acc[i * per + p].astype(jnp.bfloat16) for p in range(per)], axis=1
            )
            next_ref[:, at] = jnp.concatenate(
                [own[i * per + p].astype(next_ref.dtype) for p in range(per)], axis=1
            )
            pre = dot(w_ref[...], agg, ((1,), (0,))) + dot(b_ref[...], x_ref[:, at], ((1,), (0,)))
            fixed_ref[:, at] = jnp.maximum(pre, 0.0).astype(fixed_ref.dtype)
            adj = adj_ref[:, at]
            masked = jnp.where(z_ref[:, at] > 0, adj, jnp.zeros_like(adj))
            wg_ref[...] += dot(masked, agg, ((1,), (1,)))
            return c

        lax.fori_loop(0, nodes // LANES, chunk, 0)


def reduce_kernel(
    n, rows, scale, wg_in, ig_in, wg_out, ig_out, part, slots, total, done, s1, r1, s2, r2
):
    me = lax.axis_index("dom")
    height, width = wg_in.shape
    pieces = part.shape[0] // rows
    barrier = pltpu.get_barrier_semaphore()

    def other(j):
        return lax.rem(me + j, n)

    def greet(j, c):
        pl.semaphore_signal(barrier, inc=1, device_id=(other(j),), device_id_type=MESH)
        return c

    lax.fori_loop(1, n, greet, 0)
    part[...] = jnp.zeros_like(part)
    part[0:height, 0:width] = wg_in[...]
    part[height : 2 * height, 0 : ig_in.shape[1]] = ig_in[...]
    pl.semaphore_wait(barrier, n - 1)

    def first(p):
        return pltpu.make_async_remote_copy(
            src_ref=part.at[pl.ds(pl.multiple_of(p * rows, rows), rows)],
            dst_ref=slots.at[me],
            send_sem=s1.at[p],
            recv_sem=r1.at[me],
            device_id=(p,),
            device_id_type=MESH,
        )

    def arrived(d):
        return pltpu.make_async_remote_copy(
            src_ref=slots.at[d],
            dst_ref=slots.at[d],
            send_sem=s1.at[0],
            recv_sem=r1.at[d],
            device_id=(d,),
            device_id_type=MESH,
        )

    def second(d):
        at = pl.ds(pl.multiple_of(me * rows, rows), rows)
        return pltpu.make_async_remote_copy(
            src_ref=total,
            dst_ref=done.at[at],
            send_sem=s2.at[d],
            recv_sem=r2.at[me],
            device_id=(d,),
            device_id_type=MESH,
        )

    def second_in(p):
        at = pl.ds(pl.multiple_of(p * rows, rows), rows)
        return pltpu.make_async_remote_copy(
            src_ref=total,
            dst_ref=done.at[at],
            send_sem=s2.at[0],
            recv_sem=r2.at[p],
            device_id=(p,),
            device_id_type=MESH,
        )

    def each(count, action):
        def body(i, c):
            @pl.when(i != me)
            def _():
                action(i)

            return c

        lax.fori_loop(0, count, body, 0)

    each(pieces, lambda p: first(p).start())

    @pl.when(me < pieces)
    def _():
        own = pl.ds(pl.multiple_of(me * rows, rows), rows)
        slots[me] = part[own]
        each(n, lambda d: arrived(d).wait_recv())
        total[...] = jnp.zeros_like(total)

        def add(d, c):
            total[...] += slots[d]
            return c

        lax.fori_loop(0, n, add, 0)
        each(n, lambda d: second(d).start())
        done[own] = total[...]

    each(pieces, lambda p: second_in(p).wait_recv())
    wg_out[...] = done[0:height, 0:width] * scale
    ig_out[...] = done[height : 2 * height, 0 : ig_in.shape[1]] * scale
    each(pieces, lambda p: first(p).wait_send())

    @pl.when(me < pieces)
    def _():
        each(n, lambda d: second(d).wait_send())


def whole(array_shape):
    return pl.BlockSpec(
        array_shape, lambda i, *_: (0,) * len(array_shape), pipeline_mode=pl.Buffered(1)
    )


def per_device(
    n, z_state, inputs, adjoint, cotangent, mix_weight, input_weight, tile_values, tile_src,
    tile_dst, send_list,
):
    channels, nodes = z_state.shape
    features = inputs.shape[0]
    stored, tile, _ = tile_values.shape
    local_tiles = nodes // tile
    _, peers, cap = send_list.shape
    slots = peers * cap
    reach = peers // 2
    offsets = [r + 1 for r in range(reach)] + [-(r + 1) for r in range(reach)]
    src, dst, send = tile_src[0], tile_dst[0], send_list.reshape(-1)
    f32, bf16 = jnp.float32, jnp.bfloat16
    sds = jax.ShapeDtypeStruct
    a_spec = pl.BlockSpec((BLOCK, tile, tile), lambda i, *_: (i, 0, 0))
    piece = (channels, tile)
    wide = whole((channels, nodes))

    zout, leave, local, ig = pl.pallas_call(
        backward_kernel,
        name="backward",
        out_shape=(
            sds((slots,) + piece, bf16),
            sds((slots,) + piece, bf16),
            sds((local_tiles,) + piece, f32),
            sds((channels, features), f32),
        ),
        grid_spec=pltpu.PrefetchScalarGridSpec(
            num_scalar_prefetch=3,
            grid=(stored // BLOCK,),
            in_specs=[wide, wide, whole((features, nodes)), whole(mix_weight.shape), a_spec],
            out_specs=[
                whole((slots,) + piece),
                whole((slots,) + piece),
                whole((local_tiles,) + piece),
                whole((channels, features)),
            ],
            scratch_shapes=[
                pltpu.VMEM((channels, nodes), bf16),
                pltpu.VMEM((local_tiles + slots,) + piece, f32),
            ],
        ),
    )(src, dst, send, z_state, adjoint, inputs, mix_weight, tile_values)

    any_spec = pl.BlockSpec(memory_space=pl.ANY)
    zin, ret = pl.pallas_call(
        functools.partial(exchange_kernel, n, offsets),
        name="exchange",
        out_shape=(sds((slots,) + piece, bf16), sds((slots,) + piece, bf16)),
        in_specs=[any_spec] * 2,
        out_specs=(any_spec, any_spec),
        scratch_shapes=[
            pltpu.SemaphoreType.DMA((2, peers)),
            pltpu.SemaphoreType.DMA((2, peers)),
        ],
        compiler_params=pltpu.CompilerParams(collective_id=0, has_side_effects=True),
    )(zout, leave)

    fixed_next, adjoint_next, wg = pl.pallas_call(
        forward_kernel,
        name="forward",
        out_shape=(
            sds((channels, nodes), bf16),
            sds((channels, nodes), bf16),
            sds((channels, channels), f32),
        ),
        grid_spec=pltpu.PrefetchScalarGridSpec(
            num_scalar_prefetch=3,
            grid=(stored // BLOCK,),
            in_specs=[
                wide,
                wide,
                wide,
                whole((features, nodes)),
                whole(mix_weight.shape),
                whole(input_weight.shape),
                whole((slots,) + piece),
                whole((slots,) + piece),
                whole((local_tiles,) + piece),
                a_spec,
            ],
            out_specs=[wide, wide, whole((channels, channels))],
            scratch_shapes=[
                pltpu.VMEM((local_tiles + slots,) + piece, bf16),
                pltpu.VMEM((local_tiles,) + piece, f32),
                pltpu.VMEM((local_tiles,) + piece, f32),
            ],
        ),
    )(
        src, dst, send, z_state, adjoint, cotangent, inputs, mix_weight, input_weight, zin, ret,
        local, tile_values,
    )

    width = max(channels, features)
    units = -(-2 * channels // 8)
    rows = 8 * -(-units // n)
    pieces = -(-2 * channels // rows)
    vmem = pl.BlockSpec(memory_space=pltpu.VMEM)
    scale = 1.0 / math.sqrt(nodes * n)
    weight_grad, input_grad = pl.pallas_call(
        functools.partial(reduce_kernel, n, rows, scale),
        name="reduce",
        out_shape=(sds((channels, channels), f32), sds((channels, features), f32)),
        in_specs=[vmem] * 2,
        out_specs=(vmem, vmem),
        scratch_shapes=[
            pltpu.VMEM((pieces * rows, width), f32),
            pltpu.VMEM((n, rows, width), f32),
            pltpu.VMEM((rows, width), f32),
            pltpu.VMEM((pieces * rows, width), f32),
            pltpu.SemaphoreType.DMA((pieces,)),
            pltpu.SemaphoreType.DMA((n,)),
            pltpu.SemaphoreType.DMA((n,)),
            pltpu.SemaphoreType.DMA((pieces,)),
        ],
        compiler_params=pltpu.CompilerParams(collective_id=1, has_side_effects=True),
    )(wg, ig)
    return fixed_next, adjoint_next, weight_grad, input_grad


def solution(mesh):
    return jax.shard_map(
        functools.partial(per_device, mesh.shape["dom"]),
        mesh=mesh,
        in_specs=(
            P(None, "dom"),
            P(None, "dom"),
            P(None, "dom"),
            P(None, "dom"),
            P(),
            P(),
            P("dom", None, None),
            P("dom", None),
            P("dom", None),
            P("dom", None, None),
        ),
        out_specs=(P(None, "dom"), P(None, "dom"), P(), P()),
        check_vma=False,
    )
```
